1024 devices in a mesh: rows: 64 (over y, z_hi, core), vecs: 16 (over x, z_lo).
Axes of the slice: x: 8, y: 8, z: 8 (z_hi: 4, z_lo: 2; z = z_hi * 2 + z_lo), core: 2. Of those that a mesh axis runs over, the one named last changes fastest.
Arguments:
- eigvecs: bfloat16 [65536, 4096], P('rows', 'vecs'), may hold values from -6 to 6
- reflectors: bfloat16 [2, 65536, 1024], P(None, 'rows', 'vecs'), may hold values from -0.125 to 0.125
- factors: bfloat16 [2, 1024, 1024], replicated, as said below
Outputs:
- back_vecs: bfloat16 [65536, 4096], P('rows', 'vecs')
The draws below stay inside these ranges and needn't reach their ends.
Inputs may be any that keep to these rules, and one draw needn't show every extreme that they name: `factors`: each factor is upper triangular, its diagonal between 0.15 and 0.35.
All inputs are finite; a program needn't handle non-finite values.
Results may differ from the reference program's by a relative error of at most 0.01.
Values may be sent and summed in bfloat16 or wider, within the bound.
A program may use at most 32 MiB of HBM per device.

```python
import jax
import jax.numpy as jnp
from jax import lax

NB = 1024
M = 65536
K = 4096


def draw_factors(key, part):
    first, second = jax.random.split(jax.random.fold_in(key, 7))
    diagon = jax.random.uniform(first, (2, NB), jnp.float32, 0.15, 0.35)
    offdiag = jax.random.normal(second, (2, NB, NB), jnp.float32) * (0.3 / NB ** 0.5)
    upper = jnp.triu(offdiag, 1) + diagon[:, :, None] * jnp.eye(NB, dtype=jnp.float32)[None]
    return upper.astype(jnp.bfloat16)


def steps_of(stream_key, shape, cuts, low, high):
    def one(axis_at, shards_of):
        steps = jax.random.uniform(jax.random.fold_in(jax.random.fold_in(stream_key, 6), axis_at), (shards_of,), jnp.float32, low / len(cuts), high / len(cuts))
        return jnp.repeat(jnp.exp(steps), shape[axis_at] // shards_of).reshape((-1,) + (1,) * (len(shape) - axis_at - 1))

    factor_of = one(*cuts[0])
    for cut in cuts[1:]:
        factor_of = factor_of * one(*cut)
    return factor_of


def normal_values(key, extent, scale, bound, pieces=(), held_as=jnp.bfloat16):
    array = jax.random.normal(key, extent, jnp.float32) * scale
    if len(pieces) > 0:
        array = steps_of(key, extent, pieces, -0.22, 0.18) * array
    return jnp.clip(array, min=-bound, max=bound).astype(held_as)


def setup_inputs(seed: int = 0) -> dict:
    streams_of = jax.random.split(jax.random.key(seed), 4)
    return {
        "eigvecs": normal_values(streams_of[0], (M, K), 1.0, 6.0, ((0, 64), (1, 16))),
        "reflectors": normal_values(streams_of[1], (2, M, NB), (2 * NB) ** -0.5, 0.125, ((1, 64), (2, 16))),
        "factors": draw_factors(jax.random.fold_in(streams_of[3], 71), 0),
    }


def reference(eigvecs, reflectors, factors):
    current = eigvecs
    for which in (1, 0):
        panel = reflectors[which]
        coeff = lax.dot_general(panel, current, (((0,), (0,)), ((), ())), preferred_element_type=jnp.float32).astype(jnp.bfloat16)
        scaled = jnp.dot(factors[which], coeff, preferred_element_type=jnp.float32).astype(jnp.bfloat16)
        update = jnp.dot(panel, scaled, preferred_element_type=jnp.float32)
        current = (current.astype(jnp.float32) - update).astype(jnp.bfloat16)
    return current
```

```python
import jax
import jax.numpy as jnp
from jax import lax
from jax.experimental import pallas as pl
from jax.experimental.pallas import tpu as pltpu
from jax.sharding import PartitionSpec as P

BF = jnp.bfloat16
F32 = jnp.float32
NX, NY, NZ = 8, 8, 4
NB, R, K = 1024, 1024, 256
H = 32
KC = 128
KY = 16
T = 256

NT = (((1,), (1,)), ((), ()))
NN = (((1,), (0,)), ((), ()))
MESH = pl.DeviceIdType.MESH
FAR = (4, 3, 5, 2, 6, 1, 7)


def kernel(
    ct_ref, vt_ref, f_ref, o_ref,
    vt, fac, part, cur, csend, crecv, ysend, yrecv, zsend, zrecv, zall, full, sc,
    fsem, vsem, xs, xr, zas, zar, zbs, zbr,
    cs, cr, ys, yr, zs, zr, zgs, zgr, ygs, ygr, cgs, cgr,
):
    rows, vecs = lax.axis_index("rows"), lax.axis_index("vecs")
    y, zh, c = rows // 8, (rows // 2) % 4, rows % 2
    x, zl = vecs // 2, vecs % 2

    def at(dx=0, dzl=0, dy=0, dz=0, dc=0):
        ry = (y + dy + NY) % NY
        rz = (zh + dz + NZ) % NZ
        rc = (c + dc) % 2
        vx = (x + dx + NX) % NX
        vz = (zl + dzl) % 2
        return (ry * 8 + rz * 2 + rc, vx * 2 + vz)

    def remote(src, dst, ssem, rsem, dev):
        return pltpu.make_async_remote_copy(
            src_ref=src, dst_ref=dst, send_sem=ssem, recv_sem=rsem, device_id=dev, device_id_type=MESH
        )

    barrier = pltpu.get_barrier_semaphore()
    peers = [at(dx=1), at(dx=-1), at(dzl=1), at(dc=1)]
    peers += [at(dy=d) for d in range(1, NY)] + [at(dz=d) for d in range(1, NZ)]
    for dev in peers:
        pl.semaphore_signal(barrier, inc=1, device_id=dev, device_id_type=MESH)

    copies = []
    fcopy = [pltpu.make_async_copy(f_ref.at[p], fac.at[p], fsem.at[p]) for p in (0, 1)]
    for p in (1, 0):
        fcopy[p].start()

    def blk(ox, ozl, h):
        return ((ox + NX) % NX * 2 + ozl) * 2 + h

    own = {}
    for p in (1, 0):
        for h in (0, 1):
            own[p, h] = pltpu.make_async_copy(vt_ref.at[p, h], vt.at[p, blk(x, zl, h)], vsem.at[p, h])
            own[p, h].start()

    pl.semaphore_wait(barrier, len(peers))

    sgn = 1 - 2 * c
    ITEM = ((0, 0), (0, 1), (1, 0))
    sends = []

    def slab(p, ox, item):
        oz, h = ITEM[item]
        return vt.at[p, blk(ox, (zl + oz) % 2, h)]

    def xcopy(p, item, direction, step):
        if step == 4:
            go, src = sgn, x - 3 * sgn
        elif direction == 0:
            go, src = 1, x - (step - 1)
        else:
            go, src = -1, x + (step - 1)
        source = slab(p, src, item)
        target = source
        if step == 1 and item < 2:
            source = vt_ref.at[p, ITEM[item][1]]
        return remote(source, target, xs.at[p, item, direction, step - 1], xr.at[p, item, direction, step - 1], at(dx=go))

    def xwait(p, item, direction, step):
        xcopy(p, item, direction, step).wait_recv()

    def zacopy(p):
        return remote(vt_ref.at[p, 0], vt.at[p, blk(x, zl, 0)], zas.at[p], zar.at[p], at(dzl=1))

    def zbcopy(p, n):
        ref = slab(p, x + n, 1)
        return remote(vt_ref.at[p, 1] if n == 0 else ref, ref, zbs.at[p, n], zbr.at[p, n], at(dzl=1))

    def begin(cp):
        cp.start()
        sends.append(cp)

    def gather0(p):
        begin(zacopy(p))
        for item in (0, 1):
            for d in (0, 1):
                begin(xcopy(p, item, d, 1))
        begin(zbcopy(p, 0))

    def gather1(p):
        zacopy(p).wait_recv()
        for d in (0, 1):
            begin(xcopy(p, 2, d, 1))

    def gather_step(p, s):
        for item in (0, 1, 2):
            if s == 4:
                xwait(p, item, 0, 4)
                if item == 1:
                    begin(zbcopy(p, 4))
                continue
            for d in (0, 1):
                xwait(p, item, d, s)
                if s < 3:
                    begin(xcopy(p, item, d, s + 1))
                if item == 1:
                    begin(zbcopy(p, (8 - s) if d == 0 else s))
            if s == 3:
                begin(xcopy(p, item, 0, 4))

    def gather_end(p):
        for n in range(NX):
            zbcopy(p, n).wait_recv()
        for h in (0, 1):
            own[p, h].wait()

    def partial(p, left):
        @pl.loop(0, NB // T)
        def _(i):
            v = vt[p, pl.ds(i * (T // H), T // H)].reshape(T, R)
            part[i] = lax.dot_general(left[...], v, NT, preferred_element_type=F32)

        oc = pl.multiple_of((1 - c) * KC, KC)
        for i in range(NB // T):
            csend[p, i] = part[i, pl.ds(oc, KC), :].astype(BF)

    def corecopy(p):
        return remote(csend.at[p], crecv.at[p], cs.at[p], cr.at[p], at(dc=1))

    def ycopy(p, d):
        return remote(ysend.at[p, (y + d) % NY], yrecv.at[p, d], ys.at[p, d], yr.at[p, d], at(dy=d))

    def zcopy(p, d):
        return remote(zsend.at[p, (zh + d) % NZ], zrecv.at[p, d], zs.at[p, d], zr.at[p, d], at(dz=d))

    def zgcopy(p, d):
        return remote(zall.at[p, zh], zall.at[p, zh], zgs.at[p, d], zgr.at[p, d], at(dz=d))

    def ygcopy(p, d):
        return remote(full.at[p, c, y], full.at[p, c, y], ygs.at[p, d], ygr.at[p, d], at(dy=d))

    def cgcopy(p, d):
        ref = full.at[p, c, (y - d + NY) % NY]
        return remote(ref, ref, cgs.at[p, d], cgr.at[p, d], at(dc=1))

    def reduce_y(p):
        corecopy(p).wait_recv()
        mine = pl.multiple_of(c * KC, KC)
        for i in range(NB // T):
            s = part[i, pl.ds(mine, KC), :] + crecv[p, i].astype(F32)
            part[i, 0:KC, :] = s
            ysend[p, :, :, i * T : (i + 1) * T] = s.astype(BF).reshape(NY, KY, T)
        for d in FAR:
            begin(ycopy(p, d))

    def reduce_z(p):
        tot = [part[i, pl.ds(pl.multiple_of(y * KY, KY), KY), :] for i in range(NZ)]
        for d in range(1, NY):
            ycopy(p, d).wait_recv()
        for d in range(1, NY):
            for i in range(NZ):
                tot[i] = tot[i] + yrecv[p, d, :, i * T : (i + 1) * T].astype(F32)
        for i in range(NZ):
            part[i, 0:KY, :] = tot[i]
            zsend[p, i] = tot[i].astype(BF)
        for d in (2, 1, 3):
            begin(zcopy(p, d))

    def gather_z(p):
        tot = part[zh, 0:KY, :]
        for d in range(1, NZ):
            zcopy(p, d).wait_recv()
        for d in range(1, NZ):
            tot = tot + zrecv[p, d].astype(F32)
        zall[p, zh] = tot.astype(BF)
        for d in (2, 1, 3):
            begin(zgcopy(p, d))

    def gather_y(p):
        for d in range(1, NZ):
            src = (zh - d + NZ) % NZ
            remote(zall.at[p, src], zall.at[p, src], zgs.at[p, d], zgr.at[p, d], at(dz=d)).wait_recv()
        for i in range(NZ):
            full[p, c, y, :, i * T : (i + 1) * T] = zall[p, i]
        for d in FAR:
            begin(ygcopy(p, d))
        begin(cgcopy(p, 0))

    def gather_core(p):
        for d in (1, 7, 2, 6, 3, 5, 4):
            src = (y - d + NY) % NY
            remote(full.at[p, c, src], full.at[p, c, src], ygs.at[p, d], ygr.at[p, d], at(dy=d)).wait_recv()
            begin(cgcopy(p, d))
        for d in range(NY):
            src = (y - d + NY) % NY
            remote(full.at[p, 1 - c, src], full.at[p, 1 - c, src], cgs.at[p, d], cgr.at[p, d], at(dc=1)).wait_recv()

    def apply(p, left, out):
        fcopy[p].wait()
        coeff = full.at[p]
        for i in range(NB // T):
            a = coeff[:, :, :, i * T :].reshape(K, NB - i * T)
            b = fac[p, i * T : (i + 1) * T, i * T :]
            sc[:, i * T : (i + 1) * T] = lax.dot_general(a, b, NT, preferred_element_type=F32).astype(BF)

        @pl.loop(0, R // T)
        def _(i):
            lanes = pl.ds(pl.multiple_of(i * T, T), T)
            v = vt[p, :, :, lanes].reshape(NB, T)
            upd = lax.dot_general(sc[...], v, NN, preferred_element_type=F32)
            out[:, lanes] = (left[:, lanes].astype(F32) - upd).astype(BF)

    gather0(1)
    gather1(1)
    for s in (1, 2, 3, 4):
        gather_step(1, s)
    gather0(0)
    gather_end(1)
    partial(1, ct_ref)
    begin(corecopy(1))
    gather1(0)
    reduce_y(1)
    gather_step(0, 1)
    reduce_z(1)
    gather_step(0, 2)
    gather_z(1)
    gather_step(0, 3)
    gather_y(1)
    gather_step(0, 4)
    gather_core(1)
    apply(1, ct_ref, cur)
    gather_end(0)
    partial(0, cur)
    begin(corecopy(0))
    reduce_y(0)
    reduce_z(0)
    gather_z(0)
    gather_y(0)
    gather_core(0)
    apply(0, cur, o_ref)
    for cp in sends:
        cp.wait_send()


def body(eigvecs, reflectors, factors):
    ct = eigvecs.T
    vt = jnp.swapaxes(reflectors, 1, 2).reshape(2, 2, H, R)
    dma = pltpu.SemaphoreType.DMA
    vmem = pl.BlockSpec(memory_space=pltpu.VMEM)
    out = pl.pallas_call(
        kernel,
        out_shape=jax.ShapeDtypeStruct((K, R), BF),
        in_specs=[vmem, vmem, pl.BlockSpec(memory_space=pl.ANY)],
        out_specs=vmem,
        scratch_shapes=[
            pltpu.VMEM((2, NB // H, H, R), BF),
            pltpu.VMEM((2, NB, NB), BF),
            pltpu.VMEM((NB // T, K, T), F32),
            pltpu.VMEM((K, R), BF),
            pltpu.VMEM((2, NB // T, KC, T), BF),
            pltpu.VMEM((2, NB // T, KC, T), BF),
            pltpu.VMEM((2, NY, KY, NB), BF),
            pltpu.VMEM((2, NY, KY, NB), BF),
            pltpu.VMEM((2, NZ, KY, T), BF),
            pltpu.VMEM((2, NZ, KY, T), BF),
            pltpu.VMEM((2, NZ, KY, T), BF),
            pltpu.VMEM((2, 2, NY, KY, NB), BF),
            pltpu.VMEM((K, NB), BF),
            dma((2,)), dma((2, 2)),
            dma((2, 3, 2, 4)), dma((2, 3, 2, 4)),
            dma((2,)), dma((2,)),
            dma((2, NX)), dma((2, NX)),
            dma((2,)), dma((2,)),
            dma((2, NY)), dma((2, NY)),
            dma((2, NZ)), dma((2, NZ)),
            dma((2, NZ)), dma((2, NZ)),
            dma((2, NY)), dma((2, NY)),
            dma((2, NY)), dma((2, NY)),
        ],
        compiler_params=pltpu.CompilerParams(
            collective_id=0, has_side_effects=True, vmem_limit_bytes=40 * 1024 * 1024
        ),
        name="reflect",
    )(ct, vt, factors)
    return out.T


def solution(mesh):
    in_specs = (P("rows", "vecs"), P(None, "rows", "vecs"), P())
    out_specs = P("rows", "vecs")
    return jax.shard_map(body, mesh=mesh, in_specs=in_specs, out_specs=out_specs, check_vma=False)
```

```python
import jax
import jax.numpy as jnp
from jax import lax
from jax.experimental import pallas as pl
from jax.experimental.pallas import tpu as pltpu
from jax.sharding import PartitionSpec as P

BF = jnp.bfloat16
F32 = jnp.float32
NX, NY, NZ = 8, 8, 4
NB, R, K = 1024, 1024, 256
H = 32
KC = 128
KY = 16
T = 256

NT = (((1,), (1,)), ((), ()))
NN = (((1,), (0,)), ((), ()))
MESH = pl.DeviceIdType.MESH
PLANE = sorted(
    [(a, b) for a in range(NY) for b in range(NZ) if a or b],
    key=lambda d: (-min(d[0], NY - d[0]) - 2 * min(d[1], NZ - d[1]), d),
)


def kernel(
    e_ref, vt_ref, f_ref, o_ref,
    vt, fac, nat, ct, part, half, cur, csend, crecv, rsend, rrecv, full, sc,
    esem, fsem, osem, ssem, zsem, zbsem, x1sem, x0sem, csem, rsem, gsem, hsem,
):
    rows, vecs = lax.axis_index("rows"), lax.axis_index("vecs")
    y, zh, c = rows // 8, (rows // 2) % 4, rows % 2
    x, zl = vecs // 2, vecs % 2

    def at(dx=0, dzl=0, dy=0, dz=0, dc=0):
        ry = (y + dy) % NY
        rz = (zh + dz) % NZ
        rc = (c + dc) % 2
        vx = (x + dx + NX) % NX
        vz = (zl + dzl) % 2
        return (ry * 8 + rz * 2 + rc, vx * 2 + vz)

    def remote(src, dst, send, recv, dev):
        return pltpu.make_async_remote_copy(
            src_ref=src, dst_ref=dst, send_sem=send, recv_sem=recv, device_id=dev, device_id_type=MESH
        )

    with jax.named_scope("S_pre"):
        barrier = pltpu.get_barrier_semaphore()
        peers = [at(dx=1), at(dx=-1), at(dzl=1), at(dc=1)] + [at(dy=a, dz=b) for a, b in PLANE]
        for dev in peers:
            pl.semaphore_signal(barrier, inc=1, device_id=dev, device_id_type=MESH)

        def blk(ox, ozl, h=0):
            return ((ox + NX) % NX * 2 + ozl) * 2 + h

        ecopy = pltpu.make_async_copy(e_ref, nat, esem)
        ecopy.start()
        own = [pltpu.make_async_copy(vt_ref.at[p], vt.at[p, pl.ds(blk(x, zl), 2)], osem.at[p]) for p in (0, 1)]
        fcopy = [pltpu.make_async_copy(f_ref.at[p], fac.at[p], fsem.at[p]) for p in (0, 1)]
        for p in (1, 0):
            own[p].start()
            fcopy[p].start()

    with jax.named_scope("S_barrier"):
        pl.semaphore_wait(barrier, len(peers))

    sgn = 1 - 2 * c

    A, B, O = 0, 1, 2
    ITEM = ((0, 0), (0, 1), (1, 0))
    GROUP = {0: 0, 1: 1, 7: 1, 2: 2, 6: 2, 3: 3, 5: 3, 4: 4}

    def hop(step, direction):
        if step == 4:
            return sgn, x - 3 * sgn
        return (1, x - (step - 1)) if direction == 0 else (-1, x + (step - 1))

    def x1(item, direction, step):
        go, src = hop(step, direction)
        oz, h = ITEM[item]
        target = vt.at[1, blk(src, (zl + oz) % 2, h)]
        source = vt_ref.at[1, h] if step == 1 and item != O else target
        return remote(source, target, ssem.at[1], x1sem.at[item, direction, step - 1], at(dx=go))

    def za1():
        return remote(vt_ref.at[1, 0], vt.at[1, blk(x, zl, 0)], ssem.at[1], zsem.at[1], at(dzl=1))

    def zb1(n):
        ref = vt.at[1, blk(x + n, zl, 1)]
        return remote(vt_ref.at[1, 1] if n == 0 else ref, ref, ssem.at[1], zbsem.at[GROUP[n]], at(dzl=1))

    def start1(item, step):
        for d in (0,) if step == 4 else (0, 1):
            x1(item, d, step).start()

    def pass1(item, step):
        for d in (0,) if step == 4 else (0, 1):
            x1(item, d, step).wait_recv()
            if step < 3:
                x1(item, d, step + 1).start()
        if step == 3:
            x1(item, 0, 4).start()
        if item == B:
            for n in (4,) if step == 4 else (8 - step, step):
                zb1(n).start()

    def zb1_wait(g):
        k = 1 if g in (0, 4) else 2
        ref = vt.at[1, pl.ds(0, k)]
        remote(ref, ref, ssem.at[1], zbsem.at[g], at(dzl=1)).wait_recv()

    def x0(item, direction, step):
        go, src = hop(step, direction)
        target = vt.at[0, pl.ds(blk(src, (zl + item) % 2), 2)]
        source = vt_ref.at[0] if step == 1 and item == 0 else target
        return remote(source, target, ssem.at[0], x0sem.at[item, direction, step - 1], at(dx=go))

    def z0():
        return remote(vt_ref.at[0], vt.at[0, pl.ds(blk(x, zl), 2)], ssem.at[0], zsem.at[0], at(dzl=1))

    def start0(item):
        for d in (0, 1):
            x0(item, d, 1).start()

    def pass0(item, step):
        for d in (0,) if step == 4 else (0, 1):
            x0(item, d, step).wait_recv()
            if step < 3:
                x0(item, d, step + 1).start()
        if step == 3:
            x0(item, 0, 4).start()

    def partial(p, left, i):
        v = vt[p, pl.ds(i * (T // H), T // H)].reshape(T, R)
        part[i] = lax.dot_general(left[...], v, NT, preferred_element_type=F32)
        oc = pl.multiple_of((1 - c) * KC, KC)
        csend[p, i] = part[i, pl.ds(oc, KC), :].astype(BF)

    def corecopy(p, i, n):
        return remote(csend.at[p, i], crecv.at[p, i], ssem.at[2 + p], csem.at[p, n], at(dc=1))

    def add_core(p, i, n):
        corecopy(p, i, n).wait_recv()
        mine = pl.multiple_of(c * KC, KC)
        s = part[i, pl.ds(mine, KC), :] + crecv[p, i].astype(F32)
        half[i] = s
        rsend[p, i] = s.astype(BF).reshape(NY, KY, T)

    def scatter(p):
        for n, (a, b) in enumerate(PLANE):
            src = rsend.at[p, (zh + b) % NZ, (y + a) % NY]
            remote(src, rrecv.at[p, n], ssem.at[4 + p], rsem.at[p], at(dy=a, dz=b)).start()

    def reduce(p):
        tot = half[zh, pl.ds(pl.multiple_of(y * KY, KY), KY), :]
        ref = rrecv.at[p]
        remote(ref, ref, ssem.at[4 + p], rsem.at[p], at(dy=1)).wait_recv()
        for n in range(len(PLANE)):
            tot = tot + rrecv[p, n].astype(F32)
        full[p, c, zh, y] = tot.astype(BF)
        ref = full.at[p, c, zh, y]
        for a, b in PLANE:
            remote(ref, ref, ssem.at[6 + p], gsem.at[p, (NZ - b) % NZ], at(dy=a, dz=b)).start()

    def spread(p, b):
        ref = full.at[p, c, (zh + b) % NZ]
        got = ref if b else full.at[p, c, zh, pl.ds(0, NY - 1)]
        remote(got, got, ssem.at[6 + p], gsem.at[p, b], at(dy=1)).wait_recv()
        remote(ref, ref, ssem.at[8 + p], hsem.at[p], at(dc=1)).start()

    def spread_end(p):
        ref = full.at[p, 1 - c]
        remote(ref, ref, ssem.at[8 + p], hsem.at[p], at(dc=1)).wait_recv()

    def apply(p, left):
        fcopy[p].wait()
        for i in range(NB // T):
            acc = None
            for j in range(i, NB // T):
                a = full[p, :, j].reshape(K, T)
                b = fac[p, i * T : (i + 1) * T, j * T : (j + 1) * T]
                t = lax.dot_general(a, b, NT, preferred_element_type=F32)
                acc = t if acc is None else acc + t
            sc[:, i * T : (i + 1) * T] = acc.astype(BF)

        @pl.loop(0, R // T)
        def _(i):
            lanes = pl.ds(pl.multiple_of(i * T, T), T)
            v = vt[p, :, :, lanes].reshape(NB, T)
            upd = lax.dot_general(sc[...], v, NN, preferred_element_type=F32)
            new = (left[:, lanes].astype(F32) - upd).astype(BF)
            if p == 1:
                cur[:, lanes] = new
            else:
                o_ref[lanes, :] = new.T

    scope = jax.named_scope
    e = 1 - 2 * (x % 2)
    tiles = [(x // 2 + d + NZ) % NZ for d in (0, -e, e, 2)]

    def tile1(n):
        partial(1, ct, tiles[n])
        corecopy(1, tiles[n], n).start()
        if n > 0:
            add_core(1, tiles[n - 1], n - 1)

    with scope("S00_start"):
        za1().start()
        start1(B, 1)
        start1(A, 1)
        zb1(0).start()
    with scope("S01_transpose"):
        ecopy.wait()
        for i in range(R // T):
            ct[:, i * T : (i + 1) * T] = nat[i * T : (i + 1) * T, :].T
    with scope("S02_z"):
        za1().wait_recv()
        start1(O, 1)
    with scope("S03_BA1"):
        pass1(B, 1)
        pass1(A, 1)
    with scope("S04_OBA2"):
        pass1(O, 1)
        pass1(B, 2)
        pass1(A, 2)
    with scope("S05_tile0"):
        own[1].wait()
        zb1_wait(0)
        zb1_wait(1)
        tile1(0)
    with scope("S06_OBA3"):
        pass1(O, 2)
        pass1(B, 3)
        pass1(A, 3)
    with scope("S07_tile1"):
        zb1_wait(2)
        tile1(1)
    with scope("S08_O3"):
        pass1(O, 3)
        z0().start()
        start0(0)
    with scope("S09_BA4"):
        pass1(B, 4)
        pass1(A, 4)
    with scope("S10_tile2"):
        zb1_wait(3)
        tile1(2)
    with scope("S11_O4"):
        pass1(O, 4)
        zb1_wait(4)
    with scope("S12_tile3"):
        tile1(3)
        add_core(1, tiles[3], 3)
    with scope("S13_scatter"):
        scatter(1)
    with scope("S14_v0"):
        z0().wait_recv()
        start0(1)
        pass0(0, 1)
        pass0(1, 1)
        pass0(0, 2)
    with scope("S15_reduce"):
        reduce(1)
    with scope("S16_v0"):
        pass0(1, 2)
        pass0(0, 3)
    with scope("S17_spread"):
        spread(1, 0)
    with scope("S18_v0"):
        pass0(1, 3)
    with scope("S19_spread"):
        spread(1, 1)
        spread(1, 3)
        spread(1, 2)
        spread_end(1)
    with scope("S22_apply"):
        apply(1, ct)
    with scope("S23_v0"):
        pass0(0, 4)
        pass0(1, 4)
        own[0].wait()
    with scope("S24_partial"):
        for i in range(NZ):
            partial(0, cur, i)
            corecopy(0, i, i).start()
    with scope("S25_core"):
        for i in range(NZ):
            add_core(0, i, i)
    with scope("S26_scatter"):
        scatter(0)
    with scope("S27_reduce"):
        reduce(0)
    with scope("S28_spread"):
        for b in (0, 1, 3, 2):
            spread(0, b)
        spread_end(0)
    with scope("S29_apply"):
        apply(0, cur)
    with scope("S99_drain"):
        for p in (0, 1):
            sent = [vt.at[p, pl.ds(0, 30)], csend.at[p], rrecv.at[p], rrecv.at[p], full.at[p, c]]
            for k, ref in enumerate(sent):
                remote(ref, ref, ssem.at[2 * k + p], hsem.at[p], at(dc=1)).wait_send()


def body(eigvecs, reflectors, factors):
    vt = jnp.swapaxes(reflectors, 1, 2).reshape(2, 2, H, R)
    dma = pltpu.SemaphoreType.DMA
    hbm = pl.BlockSpec(memory_space=pltpu.HBM)
    n = len(PLANE)
    out = pl.pallas_call(
        kernel,
        out_shape=jax.ShapeDtypeStruct((R, K), BF),
        in_specs=[hbm, hbm, hbm],
        out_specs=pl.BlockSpec(memory_space=pltpu.VMEM),
        scratch_shapes=[
            pltpu.VMEM((2, NB // H, H, R), BF),
            pltpu.VMEM((2, NB, NB), BF),
            pltpu.VMEM((R, K), BF),
            pltpu.VMEM((K, R), BF),
            pltpu.VMEM((NZ, K, T), F32),
            pltpu.VMEM((NZ, KC, T), F32),
            pltpu.VMEM((K, R), BF),
            pltpu.VMEM((2, NZ, KC, T), BF),
            pltpu.VMEM((2, NZ, KC, T), BF),
            pltpu.VMEM((2, NZ, NY, KY, T), BF),
            pltpu.VMEM((2, n, KY, T), BF),
            pltpu.VMEM((2, 2, NZ, NY, KY, T), BF),
            pltpu.VMEM((K, NB), BF),
            dma(()), dma((2,)), dma((2,)),
            dma((10,)),
            dma((2,)), dma((5,)),
            dma((3, 2, 4)), dma((2, 2, 4)),
            dma((2, NZ)), dma((2,)), dma((2, NZ)), dma((2,)),
        ],
        compiler_params=pltpu.CompilerParams(
            collective_id=0, has_side_effects=True, vmem_limit_bytes=60 * 1024 * 1024
        ),
        name="reflect",
    )(eigvecs, vt, factors)
    return out


def solution(mesh):
    in_specs = (P("rows", "vecs"), P(None, "rows", "vecs"), P())
    out_specs = P("rows", "vecs")
    return jax.shard_map(body, mesh=mesh, in_specs=in_specs, out_specs=out_specs, check_vma=False)
```

```python
import jax
import jax.numpy as jnp
from jax import lax
from jax.experimental import pallas as pl
from jax.experimental.pallas import tpu as pltpu
from jax.sharding import PartitionSpec as P

BF = jnp.bfloat16
F32 = jnp.float32
NX, NY, NZ = 8, 8, 4
NB, R, K = 1024, 1024, 256
H = 16
U = 4
FIRST = (3, 2)
SENT = [(1 + 14) * n + (7 + 8) * (U - n) for n in FIRST]
KH = 128
KC = 64
KY = 16
T = 256
TL = 128

NT = (((1,), (1,)), ((), ()))
NN = (((1,), (0,)), ((), ()))
MESH = pl.DeviceIdType.MESH
PLANE = sorted(
    [(a, b) for a in range(NY) for b in range(NZ) if a or b],
    key=lambda d: (-min(d[0], NY - d[0]) - 2 * min(d[1], NZ - d[1]), d),
)


def kernel(
    e_ref, vt_ref, f_ref, o_ref,
    vt, fac, nat, ct, part, half, cur, csend, crecv, rsend, rrecv, full, sc,
    esem, fsem, osem, ssem, zsem, zbsem, xsem, csem, rsem, gsem, hsem, in_z, in_y,
):
    rows, vecs = lax.axis_index("rows"), lax.axis_index("vecs")
    y, zh, c = rows // 8, (rows // 2) % 4, rows % 2
    x, zl = vecs // 2, vecs % 2

    def at(dx=0, dzl=0, dy=0, dz=0, dc=0):
        ry = (y + dy) % NY
        rz = (zh + dz) % NZ
        rc = (c + dc) % 2
        vx = (x + dx + NX) % NX
        vz = (zl + dzl) % 2
        return (ry * 8 + rz * 2 + rc, vx * 2 + vz)

    def remote(src, dst, send, recv, dev):
        return pltpu.make_async_remote_copy(
            src_ref=src, dst_ref=dst, send_sem=send, recv_sem=recv, device_id=dev, device_id_type=MESH
        )

    with jax.named_scope("S_pre"):
        barrier = pltpu.get_barrier_semaphore()
        peers = [at(dx=1), at(dx=-1), at(dzl=1), at(dc=1), at(dy=1), at(dy=-1), at(dz=1), at(dz=-1)]
        for dev in peers:
            pl.semaphore_signal(barrier, inc=1, device_id=dev, device_id_type=MESH)

        def blk(ox, ozl):
            return ((ox + NX) % NX * 2 + ozl) * U

        ecopy = pltpu.make_async_copy(e_ref, nat, esem)
        ecopy.start()
        own = [pltpu.make_async_copy(vt_ref.at[p], vt.at[p, pl.ds(blk(x, zl), U)], osem.at[p]) for p in (0, 1)]
        fcopy = [pltpu.make_async_copy(f_ref.at[p], fac.at[p], fsem.at[p]) for p in (0, 1)]
        for p in (1, 0):
            own[p].start()
            fcopy[p].start()

    with jax.named_scope("S_barrier"):
        pl.semaphore_wait(barrier, len(peers))

    def tell(sem, dev):
        pl.semaphore_signal(sem, inc=1, device_id=dev, device_id_type=MESH)

    def hear(n):
        if n == 0:
            tell(in_z, at(dz=-1))
            return
        if n == 1:
            pl.semaphore_wait(in_z, 1)
        else:
            for d in (0, 1):
                pl.semaphore_wait(in_y.at[n - 2, d], 1)
        if n <= NY // 2:
            tell(in_y.at[n - 1, 0], at(dy=1))
            tell(in_y.at[n - 1, 1], at(dy=-1))

    sgn = 1 - 2 * c

    A, B, O = 0, 1, 2
    GROUP = {0: 0, 1: 1, 7: 1, 2: 2, 6: 2, 3: 3, 5: 3, 4: 4}

    def units(p, item):
        return (FIRST[p], U - FIRST[p]) if item == B else (0, FIRST[p])

    def hop(step, direction):
        if step == 4:
            return sgn, x - 3 * sgn
        return (1, x - (step - 1)) if direction == 0 else (-1, x + (step - 1))

    def xcopy(p, item, direction, step):
        go, src = hop(step, direction)
        at_unit, n = units(p, item)
        target = vt.at[p, pl.ds(blk(src, (zl + (item == O)) % 2) + at_unit, n)]
        source = vt_ref.at[p, at_unit : at_unit + n] if step == 1 and item != O else target
        return remote(source, target, ssem.at[p], xsem.at[p, item, direction, step - 1], at(dx=go))

    def za(p):
        return remote(vt_ref.at[p, : FIRST[p]], vt.at[p, pl.ds(blk(x, zl), FIRST[p])], ssem.at[p], zsem.at[p], at(dzl=1))

    def zbsem_of(p, g):
        return zbsem.at[g if p == 1 else 5]

    def zb(p, k):
        at_unit, n = units(p, B)
        ref = vt.at[p, pl.ds(blk(x + k, zl) + at_unit, n)]
        return remote(vt_ref.at[p, at_unit:] if k == 0 else ref, ref, ssem.at[p], zbsem_of(p, GROUP[k]), at(dzl=1))

    def start(p, item):
        for d in (0, 1):
            xcopy(p, item, d, 1).start()

    def forward(p, item, step):
        for d in (0,) if step == 4 else (0, 1):
            xcopy(p, item, d, step).wait_recv()
            if step < 3:
                xcopy(p, item, d, step + 1).start()
        if step == 3:
            xcopy(p, item, 0, 4).start()
        if item == B:
            for k in (4,) if step == 4 else (8 - step, step):
                zb(p, k).start()

    def zb_wait(p, g, blocks):
        ref = vt.at[p, pl.ds(0, blocks * (U - FIRST[p]))]
        remote(ref, ref, ssem.at[p], zbsem_of(p, g), at(dzl=1)).wait_recv()

    def mine(hf, who):
        return pl.ds(pl.multiple_of(hf * KH + who * KC, KC), KC)

    def partial(p, left, i):
        v = vt[p, pl.ds(i * (T // H), T // H)].reshape(T, R)
        part[i] = lax.dot_general(left[...], v, NT, preferred_element_type=F32)

    def outgoing(p, i, hf):
        csend[p, i, hf] = part[i, mine(hf, 1 - c), :].astype(BF)

    def core1(i, n):
        return remote(csend.at[1, i], crecv.at[1, i], ssem.at[3], csem.at[n], at(dc=1))

    def core0(i, hf):
        return remote(csend.at[0, i, hf], crecv.at[0, i, hf], ssem.at[2], csem.at[NZ + hf], at(dc=1))

    def add_core(p, i, hf):
        s = part[i, mine(hf, c), :] + crecv[p, i, hf].astype(F32)
        for q in (0, 1):
            t = s[:, q * TL : (q + 1) * TL].reshape(NY // 2, KY, TL)
            half[hf, i, q * (NY // 2) : (q + 1) * (NY // 2)] = t
            rsend[p, hf, i, q * (NY // 2) : (q + 1) * (NY // 2)] = t.astype(BF)

    def scatter(p, hf):
        for n, (a, b) in enumerate(PLANE):
            src = rsend.at[p, hf, (zh + b) % NZ, (y + a) % NY]
            remote(src, rrecv.at[p, hf, n], ssem.at[4 + 2 * p + hf], rsem.at[p, hf], at(dy=a, dz=b)).start()

    def reduce(p, hf):
        tot = half[hf, zh, y]
        ref = rrecv.at[p, hf]
        remote(ref, ref, ssem.at[4 + 2 * p + hf], rsem.at[p, hf], at(dy=1)).wait_recv()
        for n in range(len(PLANE)):
            tot = tot + rrecv[p, hf, n].astype(F32)
        full[p, hf, c, zh, y] = tot.astype(BF)
        ref = full.at[p, hf, c, zh, y]
        for a, b in PLANE:
            remote(ref, ref, ssem.at[8 + 2 * p + hf], gsem.at[p, hf, (NZ - b) % NZ], at(dy=a, dz=b)).start()

    def spread(p, hf):
        for b in (0, 1, 3, 2):
            ref = full.at[p, hf, c, (zh + b) % NZ]
            got = ref if b else full.at[p, hf, c, zh, pl.ds(0, NY - 1)]
            remote(got, got, ssem.at[8 + 2 * p + hf], gsem.at[p, hf, b], at(dy=1)).wait_recv()
            remote(ref, ref, ssem.at[12 + 2 * p + hf], hsem.at[p, hf], at(dc=1)).start()

    def spread_end(p, hf):
        ref = full.at[p, hf, 1 - c]
        remote(ref, ref, ssem.at[12 + 2 * p + hf], hsem.at[p, hf], at(dc=1)).wait_recv()

    def apply(p, left):
        fcopy[p].wait()
        coeff = []
        for j in range(NZ):
            w = full[p, :, :, j]
            coeff.append(jnp.concatenate([w[:, :, : NY // 2].reshape(K, TL), w[:, :, NY // 2 :].reshape(K, TL)], axis=1))
        for i in range(NB // T):
            acc = None
            for j in range(i, NB // T):
                b = fac[p, i * T : (i + 1) * T, j * T : (j + 1) * T]
                t = lax.dot_general(coeff[j], b, NT, preferred_element_type=F32)
                acc = t if acc is None else acc + t
            sc[:, i * T : (i + 1) * T] = acc.astype(BF)

        @pl.loop(0, R // T)
        def _(i):
            lanes = pl.ds(pl.multiple_of(i * T, T), T)
            v = vt[p, :, :, lanes].reshape(NB, T)
            upd = lax.dot_general(sc[...], v, NN, preferred_element_type=F32)
            new = (left[:, lanes].astype(F32) - upd).astype(BF)
            if p == 1:
                cur[:, lanes] = new
            else:
                o_ref[lanes, :] = new.T

    scope = jax.named_scope
    e = 1 - 2 * (x % 2)
    tiles = [(x // 2 + d + NZ) % NZ for d in (0, -e, e, 2)]

    def add1(n):
        core1(tiles[n], n).wait_recv()
        for hf in (0, 1):
            add_core(1, tiles[n], hf)

    def tile1(n):
        partial(1, ct, tiles[n])
        for hf in (0, 1):
            outgoing(1, tiles[n], hf)
        core1(tiles[n], n).start()
        if n > 0:
            add1(n - 1)

    def partial0():
        @pl.loop(0, NZ)
        def _(i):
            partial(0, cur, i)

        for hf in (0, 1):
            for i in range(NZ):
                outgoing(0, i, hf)
                core0(i, hf).start()

    def add0(hf):
        ref = crecv.at[0, pl.ds(0, 2)]
        remote(ref, ref, ssem.at[2], csem.at[NZ + hf], at(dc=1)).wait_recv()
        for i in range(NZ):
            add_core(0, i, hf)

    with scope("S00_start"):
        za(1).start()
        start(1, B)
        start(1, A)
        zb(1, 0).start()
        hear(0)
    with scope("S01_transpose"):
        ecopy.wait()
        for i in range(R // T):
            ct[:, i * T : (i + 1) * T] = nat[i * T : (i + 1) * T, :].T
    with scope("S02_z"):
        za(1).wait_recv()
        start(1, O)
    with scope("S03_BA1"):
        forward(1, B, 1)
        forward(1, A, 1)
        hear(1)
    with scope("S04_OBA2"):
        forward(1, O, 1)
        forward(1, B, 2)
        forward(1, A, 2)
        hear(2)
    with scope("S05_tile0"):
        own[1].wait()
        zb_wait(1, 0, 1)
        zb_wait(1, 1, 2)
        tile1(0)
    with scope("S06_OBA3"):
        forward(1, O, 2)
        forward(1, B, 3)
        forward(1, A, 3)
        hear(3)
    with scope("S07_tile1"):
        zb_wait(1, 2, 2)
        tile1(1)
    with scope("S08_O3"):
        forward(1, O, 3)
    with scope("S09_BA4"):
        forward(1, B, 4)
        za(0).start()
        forward(1, A, 4)
        hear(4)
    with scope("S10_tile2"):
        zb_wait(1, 3, 2)
        tile1(2)
    with scope("S11_O4"):
        forward(1, O, 4)
        start(0, B)
        start(0, A)
        zb(0, 0).start()
        zb_wait(1, 4, 1)
    with scope("S12_tile3"):
        tile1(3)
        add1(3)
    with scope("S13_scatter"):
        hear(5)
        scatter(1, 0)
        scatter(1, 1)
    with scope("S14_v0"):
        za(0).wait_recv()
        start(0, O)
        forward(0, B, 1)
        forward(0, A, 1)
        forward(0, O, 1)
    with scope("S15_reduceA"):
        reduce(1, 0)
    with scope("S16_v0"):
        forward(0, B, 2)
        forward(0, A, 2)
    with scope("S17_reduceB"):
        reduce(1, 1)
    with scope("S18_v0"):
        forward(0, O, 2)
        forward(0, B, 3)
        forward(0, A, 3)
    with scope("S19_spreadA"):
        spread(1, 0)
    with scope("S20_v0"):
        forward(0, O, 3)
    with scope("S21_spreadB"):
        spread(1, 1)
    with scope("S22_v0"):
        forward(0, B, 4)
    with scope("S23_spreadend"):
        spread_end(1, 0)
        spread_end(1, 1)
    with scope("S24_apply"):
        apply(1, ct)
    with scope("S25_v0"):
        forward(0, A, 4)
        forward(0, O, 4)
        zb_wait(0, 5, NX)
        own[0].wait()
    with scope("S26_partial"):
        partial0()
    with scope("S27_scatter"):
        for hf in (0, 1):
            add0(hf)
            scatter(0, hf)
    with scope("S30_reduceA"):
        reduce(0, 0)
    with scope("S31_reduceB"):
        reduce(0, 1)
    with scope("S32_spreadA"):
        spread(0, 0)
    with scope("S33_spreadB"):
        spread(0, 1)
    with scope("S34_spreadend"):
        spread_end(0, 0)
        spread_end(0, 1)
    with scope("S35_apply"):
        apply(0, cur)
    with scope("S99_drain"):
        sent = [(1, vt.at[1, pl.ds(0, SENT[1])]), (0, vt.at[0, pl.ds(0, SENT[0])])] + [(2 + p, csend.at[p]) for p in (0, 1)]
        for p in (0, 1):
            for hf in (0, 1):
                m = 2 * p + hf
                sent += [(4 + m, rrecv.at[p, hf]), (8 + m, rrecv.at[p, hf]), (12 + m, full.at[p, hf, c])]
        for m, ref in sent:
            remote(ref, ref, ssem.at[m], hsem.at[0, 0], at(dc=1)).wait_send()


def body(eigvecs, reflectors, factors):
    vt = jnp.swapaxes(reflectors, 1, 2).reshape(2, U, H, R)
    dma = pltpu.SemaphoreType.DMA
    hbm = pl.BlockSpec(memory_space=pltpu.HBM)
    n = len(PLANE)
    out = pl.pallas_call(
        kernel,
        out_shape=pltpu.VMEM((R, K), BF),
        in_specs=[hbm, hbm, hbm],
        out_specs=pl.BlockSpec(memory_space=pltpu.VMEM),
        scratch_shapes=[
            pltpu.VMEM((2, NB // H, H, R), BF),
            pltpu.VMEM((2, NB, NB), BF),
            pltpu.VMEM((R, K), BF),
            pltpu.VMEM((K, R), BF),
            pltpu.VMEM((NZ, K, T), F32),
            pltpu.VMEM((2, NZ, NY, KY, TL), F32),
            pltpu.VMEM((K, R), BF),
            pltpu.VMEM((2, NZ, 2, KC, T), BF),
            pltpu.VMEM((2, NZ, 2, KC, T), BF),
            pltpu.VMEM((2, 2, NZ, NY, KY, TL), BF),
            pltpu.VMEM((2, 2, n, KY, TL), BF),
            pltpu.VMEM((2, 2, 2, NZ, NY, KY, TL), BF),
            pltpu.VMEM((K, NB), BF),
            dma(()), dma((2,)), dma((2,)),
            dma((16,)),
            dma((2,)), dma((6,)),
            dma((2, 3, 2, 4)),
            dma((NZ + 2,)), dma((2, 2)), dma((2, 2, NZ)), dma((2, 2)),
            pltpu.SemaphoreType.REGULAR, pltpu.SemaphoreType.REGULAR((NY // 2, 2)),
        ],
        compiler_params=pltpu.CompilerParams(
            collective_id=0, has_side_effects=True, vmem_limit_bytes=60 * 1024 * 1024
        ),
        name="reflect",
    )(eigvecs, vt, factors)
    return out


def solution(mesh):
    in_specs = (P("rows", "vecs"), P(None, "rows", "vecs"), P())
    out_specs = P("rows", "vecs")
    return jax.shard_map(body, mesh=mesh, in_specs=in_specs, out_specs=out_specs, check_vma=False)
```

```python
import jax
import jax.numpy as jnp
from jax import lax
from jax.experimental import pallas as pl
from jax.experimental.pallas import tpu as pltpu
from jax.sharding import PartitionSpec as P

BF = jnp.bfloat16
F32 = jnp.float32
NX, NY, NZ = 8, 8, 4
NB, R, K = 1024, 1024, 256
H = 16
U = 4
FIRST = (3, 2)
SENT = [(1 + 14) * n + (7 + 8) * (U - n) for n in FIRST]
KH = 128
KC = 64
KY = 16
T = 256
TL = 128

NT = (((1,), (1,)), ((), ()))
NN = (((1,), (0,)), ((), ()))
MESH = pl.DeviceIdType.MESH
PLANE = sorted(
    [(a, b) for a in range(NY) for b in range(NZ) if a or b],
    key=lambda d: (-min(d[0], NY - d[0]) - 2 * min(d[1], NZ - d[1]), d),
)


def kernel(
    e_ref, vt_ref, f_ref, o_ref,
    vt, fac, nat, ct, part, half, cur, csend, crecv, rsend, rrecv, full, sc,
    esem, fsem, osem, ssem, zsem, zbsem, xsem, csem, rsem, gsem, hsem, in_z, in_y,
):
    rows, vecs = lax.axis_index("rows"), lax.axis_index("vecs")
    y, zh, c = rows // 8, (rows // 2) % 4, rows % 2
    x, zl = vecs // 2, vecs % 2

    def at(dx=0, dzl=0, dy=0, dz=0, dc=0):
        ry = (y + dy) % NY
        rz = (zh + dz) % NZ
        rc = (c + dc) % 2
        vx = (x + dx + NX) % NX
        vz = (zl + dzl) % 2
        return (ry * 8 + rz * 2 + rc, vx * 2 + vz)

    def remote(src, dst, send, recv, dev):
        return pltpu.make_async_remote_copy(
            src_ref=src, dst_ref=dst, send_sem=send, recv_sem=recv, device_id=dev, device_id_type=MESH
        )

    with jax.named_scope("S_pre"):
        barrier = pltpu.get_barrier_semaphore()
        peers = [at(dx=1), at(dx=-1), at(dzl=1), at(dc=1), at(dy=1), at(dy=-1), at(dz=1), at(dz=-1)]
        for dev in peers:
            pl.semaphore_signal(barrier, inc=1, device_id=dev, device_id_type=MESH)

        def blk(ox, ozl):
            return ((ox + NX) % NX * 2 + ozl) * U

        ecopy = pltpu.make_async_copy(e_ref, nat, esem)
        ecopy.start()
        own = [pltpu.make_async_copy(vt_ref.at[p], vt.at[p, pl.ds(blk(x, zl), U)], osem.at[p]) for p in (0, 1)]
        fcopy = [pltpu.make_async_copy(f_ref.at[p], fac.at[p], fsem.at[p]) for p in (0, 1)]
        for p in (1, 0):
            own[p].start()
            fcopy[p].start()

    with jax.named_scope("S_barrier"):
        pl.semaphore_wait(barrier, len(peers))

    def tell(sem, dev):
        pl.semaphore_signal(sem, inc=1, device_id=dev, device_id_type=MESH)

    def hear(n):
        if n == 0:
            tell(in_z, at(dz=-1))
            return
        if n == 1:
            pl.semaphore_wait(in_z, 1)
        else:
            for d in (0, 1):
                pl.semaphore_wait(in_y.at[n - 2, d], 1)
        if n <= NY // 2:
            tell(in_y.at[n - 1, 0], at(dy=1))
            tell(in_y.at[n - 1, 1], at(dy=-1))

    sgn = 1 - 2 * c

    A, B, O = 0, 1, 2
    GROUP = {0: 0, 1: 1, 7: 1, 2: 2, 6: 2, 3: 3, 5: 3, 4: 4}

    def units(p, item):
        return (FIRST[p], U - FIRST[p]) if item == B else (0, FIRST[p])

    def hop(step, direction):
        if step == 4:
            return sgn, x - 3 * sgn
        return (1, x - (step - 1)) if direction == 0 else (-1, x + (step - 1))

    def xcopy(p, item, direction, step):
        go, src = hop(step, direction)
        at_unit, n = units(p, item)
        target = vt.at[p, pl.ds(blk(src, (zl + (item == O)) % 2) + at_unit, n)]
        source = vt_ref.at[p, at_unit : at_unit + n] if step == 1 and item != O else target
        return remote(source, target, ssem.at[p], xsem.at[p, item, direction, step - 1], at(dx=go))

    def za(p):
        return remote(vt_ref.at[p, : FIRST[p]], vt.at[p, pl.ds(blk(x, zl), FIRST[p])], ssem.at[p], zsem.at[p], at(dzl=1))

    def zbsem_of(p, g):
        return zbsem.at[g if p == 1 else 5]

    def zb(p, k):
        at_unit, n = units(p, B)
        ref = vt.at[p, pl.ds(blk(x + k, zl) + at_unit, n)]
        return remote(vt_ref.at[p, at_unit:] if k == 0 else ref, ref, ssem.at[p], zbsem_of(p, GROUP[k]), at(dzl=1))

    def start(p, item):
        for d in (0, 1):
            xcopy(p, item, d, 1).start()

    def forward(p, item, step):
        for d in (0,) if step == 4 else (0, 1):
            xcopy(p, item, d, step).wait_recv()
            if step < 3:
                xcopy(p, item, d, step + 1).start()
        if step == 3:
            xcopy(p, item, 0, 4).start()
        if item == B:
            for k in (4,) if step == 4 else (8 - step, step):
                zb(p, k).start()

    def zb_wait(p, g, blocks):
        ref = vt.at[p, pl.ds(0, blocks * (U - FIRST[p]))]
        remote(ref, ref, ssem.at[p], zbsem_of(p, g), at(dzl=1)).wait_recv()

    def mine(hf, who):
        return pl.ds(pl.multiple_of(hf * KH + who * KC, KC), KC)

    def partial(p, left, i):
        v = vt[p, pl.ds(i * (T // H), T // H)].reshape(T, R)
        part[i] = lax.dot_general(left[...], v, NT, preferred_element_type=F32)

    def outgoing(p, i, hf):
        csend[p, i, hf] = part[i, mine(hf, 1 - c), :].astype(BF)

    def core1(i, n):
        return remote(csend.at[1, i], crecv.at[1, i], ssem.at[3], csem.at[n], at(dc=1))

    def core0(i, hf):
        return remote(csend.at[0, i, hf], crecv.at[0, i, hf], ssem.at[2], csem.at[NZ + hf], at(dc=1))

    def add_core(p, i, hf):
        s = part[i, mine(hf, c), :] + crecv[p, i, hf].astype(F32)
        for q in (0, 1):
            t = s[:, q * TL : (q + 1) * TL].reshape(NY // 2, KY, TL)
            half[hf, i, q * (NY // 2) : (q + 1) * (NY // 2)] = t
            rsend[p, hf, i, q * (NY // 2) : (q + 1) * (NY // 2)] = t.astype(BF)

    def scatter(p, hf):
        for n, (a, b) in enumerate(PLANE):
            src = rsend.at[p, hf, (zh + b) % NZ, (y + a) % NY]
            remote(src, rrecv.at[p, hf, n], ssem.at[4 + 2 * p + hf], rsem.at[p, hf], at(dy=a, dz=b)).start()

    def reduce(p, hf):
        tot = half[hf, zh, y]
        ref = rrecv.at[p, hf]
        remote(ref, ref, ssem.at[4 + 2 * p + hf], rsem.at[p, hf], at(dy=1)).wait_recv()
        for n in range(len(PLANE)):
            tot = tot + rrecv[p, hf, n].astype(F32)
        full[p, hf, c, zh, y] = tot.astype(BF)
        ref = full.at[p, hf, c, zh, y]
        for a, b in PLANE:
            remote(ref, ref, ssem.at[8 + 2 * p + hf], gsem.at[p, hf, (NZ - b) % NZ], at(dy=a, dz=b)).start()

    def spread(p, hf):
        for b in (0, 1, 3, 2):
            ref = full.at[p, hf, c, (zh + b) % NZ]
            got = ref if b else full.at[p, hf, c, zh, pl.ds(0, NY - 1)]
            remote(got, got, ssem.at[8 + 2 * p + hf], gsem.at[p, hf, b], at(dy=1)).wait_recv()
            remote(ref, ref, ssem.at[12 + 2 * p + hf], hsem.at[p, hf], at(dc=1)).start()

    def spread_end(p, hf):
        ref = full.at[p, hf, 1 - c]
        remote(ref, ref, ssem.at[12 + 2 * p + hf], hsem.at[p, hf], at(dc=1)).wait_recv()

    def apply(p, left):
        fcopy[p].wait()
        coeff = []
        for j in range(NZ):
            w = full[p, :, :, j]
            coeff.append(jnp.concatenate([w[:, :, : NY // 2].reshape(K, TL), w[:, :, NY // 2 :].reshape(K, TL)], axis=1))
        for i in range(NB // T):
            acc = None
            for j in range(i, NB // T):
                b = fac[p, i * T : (i + 1) * T, j * T : (j + 1) * T]
                t = lax.dot_general(coeff[j], b, NT, preferred_element_type=F32)
                acc = t if acc is None else acc + t
            sc[:, i * T : (i + 1) * T] = acc.astype(BF)

        for i in range(R // T):
            lanes = slice(i * T, (i + 1) * T)
            v = vt[p, :, :, lanes].reshape(NB, T)
            upd = lax.dot_general(sc[...], v, NN, preferred_element_type=F32)
            new = (left[:, lanes].astype(F32) - upd).astype(BF)
            if p == 1:
                cur[:, lanes] = new
            else:
                o_ref[lanes, :] = new.T

    scope = jax.named_scope
    e = 1 - 2 * (x % 2)
    tiles = [(x // 2 + d + NZ) % NZ for d in (0, -e, e, 2)]

    def add1(n):
        core1(tiles[n], n).wait_recv()
        for hf in (0, 1):
            add_core(1, tiles[n], hf)

    def tile1(n):
        partial(1, ct, tiles[n])
        for hf in (0, 1):
            outgoing(1, tiles[n], hf)
        core1(tiles[n], n).start()
        if n > 0:
            add1(n - 1)

    def partial0():
        for i in range(NZ):
            partial(0, cur, i)

        for hf in (0, 1):
            for i in range(NZ):
                outgoing(0, i, hf)
                core0(i, hf).start()

    def add0(hf):
        ref = crecv.at[0, pl.ds(0, 2)]
        remote(ref, ref, ssem.at[2], csem.at[NZ + hf], at(dc=1)).wait_recv()
        for i in range(NZ):
            add_core(0, i, hf)

    with scope("S00_start"):
        za(1).start()
        start(1, B)
        start(1, A)
        zb(1, 0).start()
        hear(0)
    with scope("S01_transpose"):
        ecopy.wait()
        for i in range(R // T):
            ct[:, i * T : (i + 1) * T] = nat[i * T : (i + 1) * T, :].T
    with scope("S02_z"):
        za(1).wait_recv()
        start(1, O)
    with scope("S03_BA1"):
        forward(1, B, 1)
        forward(1, A, 1)
        hear(1)
    with scope("S04_OBA2"):
        forward(1, O, 1)
        forward(1, B, 2)
        forward(1, A, 2)
        hear(2)
    with scope("S05_tile0"):
        own[1].wait()
        zb_wait(1, 0, 1)
        zb_wait(1, 1, 2)
        tile1(0)
    with scope("S06_OBA3"):
        forward(1, O, 2)
        forward(1, B, 3)
        forward(1, A, 3)
        hear(3)
    with scope("S07_tile1"):
        zb_wait(1, 2, 2)
        tile1(1)
    with scope("S08_O3"):
        forward(1, O, 3)
    with scope("S09_BA4"):
        forward(1, B, 4)
        za(0).start()
        forward(1, A, 4)
        hear(4)
    with scope("S10_tile2"):
        zb_wait(1, 3, 2)
        tile1(2)
    with scope("S11_O4"):
        forward(1, O, 4)
        start(0, B)
        start(0, A)
        zb(0, 0).start()
        zb_wait(1, 4, 1)
    with scope("S12_tile3"):
        tile1(3)
        add1(3)
    with scope("S13_scatter"):
        hear(5)
        scatter(1, 0)
        scatter(1, 1)
    with scope("S14_v0"):
        za(0).wait_recv()
        start(0, O)
        forward(0, B, 1)
        forward(0, A, 1)
        forward(0, O, 1)
    with scope("S15_reduceA"):
        reduce(1, 0)
    with scope("S16_v0"):
        forward(0, B, 2)
        forward(0, A, 2)
    with scope("S17_reduceB"):
        reduce(1, 1)
    with scope("S18_v0"):
        forward(0, O, 2)
        forward(0, B, 3)
        forward(0, A, 3)
        forward(0, O, 3)
    with scope("S19_spreadA"):
        spread(1, 0)
    with scope("S21_spreadB"):
        spread(1, 1)
    with scope("S22_v0"):
        forward(0, B, 4)
    with scope("S23_spreadend"):
        spread_end(1, 0)
        spread_end(1, 1)
    with scope("S24_apply"):
        apply(1, ct)
    with scope("S25_v0"):
        forward(0, A, 4)
        forward(0, O, 4)
        zb_wait(0, 5, NX)
        own[0].wait()
    with scope("S26_partial"):
        partial0()
    with scope("S27_scatter"):
        for hf in (0, 1):
            add0(hf)
            scatter(0, hf)
    with scope("S30_reduceA"):
        reduce(0, 0)
    with scope("S31_reduceB"):
        reduce(0, 1)
    with scope("S32_spreadA"):
        spread(0, 0)
    with scope("S33_spreadB"):
        spread(0, 1)
    with scope("S34_spreadend"):
        spread_end(0, 0)
        spread_end(0, 1)
    with scope("S35_apply"):
        apply(0, cur)
    with scope("S99_drain"):
        sent = [(1, vt.at[1, pl.ds(0, SENT[1])]), (0, vt.at[0, pl.ds(0, SENT[0])])] + [(2 + p, csend.at[p]) for p in (0, 1)]
        for p in (0, 1):
            for hf in (0, 1):
                m = 2 * p + hf
                sent += [(4 + m, rrecv.at[p, hf]), (8 + m, rrecv.at[p, hf]), (12 + m, full.at[p, hf, c])]
        for m, ref in sent:
            remote(ref, ref, ssem.at[m], hsem.at[0, 0], at(dc=1)).wait_send()


def body(eigvecs, reflectors, factors):
    vt = jnp.swapaxes(reflectors, 1, 2).reshape(2, U, H, R)
    dma = pltpu.SemaphoreType.DMA
    hbm = pl.BlockSpec(memory_space=pltpu.HBM)
    n = len(PLANE)
    out = pl.pallas_call(
        kernel,
        out_shape=pltpu.VMEM((R, K), BF),
        in_specs=[hbm, hbm, hbm],
        out_specs=pl.BlockSpec(memory_space=pltpu.VMEM),
        scratch_shapes=[
            pltpu.VMEM((2, NB // H, H, R), BF),
            pltpu.VMEM((2, NB, NB), BF),
            pltpu.VMEM((R, K), BF),
            pltpu.VMEM((K, R), BF),
            pltpu.VMEM((NZ, K, T), F32),
            pltpu.VMEM((2, NZ, NY, KY, TL), F32),
            pltpu.VMEM((K, R), BF),
            pltpu.VMEM((2, NZ, 2, KC, T), BF),
            pltpu.VMEM((2, NZ, 2, KC, T), BF),
            pltpu.VMEM((2, 2, NZ, NY, KY, TL), BF),
            pltpu.VMEM((2, 2, n, KY, TL), BF),
            pltpu.VMEM((2, 2, 2, NZ, NY, KY, TL), BF),
            pltpu.VMEM((K, NB), BF),
            dma(()), dma((2,)), dma((2,)),
            dma((16,)),
            dma((2,)), dma((6,)),
            dma((2, 3, 2, 4)),
            dma((NZ + 2,)), dma((2, 2)), dma((2, 2, NZ)), dma((2, 2)),
            pltpu.SemaphoreType.REGULAR, pltpu.SemaphoreType.REGULAR((NY // 2, 2)),
        ],
        compiler_params=pltpu.CompilerParams(
            collective_id=0, has_side_effects=True, vmem_limit_bytes=60 * 1024 * 1024
        ),
        name="reflect",
    )(eigvecs, vt, factors)
    return out


def solution(mesh):
    in_specs = (P("rows", "vecs"), P(None, "rows", "vecs"), P())
    out_specs = P("rows", "vecs")
    return jax.shard_map(body, mesh=mesh, in_specs=in_specs, out_specs=out_specs, check_vma=False)
```
